512 devices in a mesh: rows: 128 (over z, y, core), grp: 4 (over x).
Axes of the slice: x: 4, y: 4, z: 16, core: 2. Of those that a mesh axis runs over, the one named last changes fastest.
Arguments:
- rhs: float32 [3, 128, 4, 2, 512], P(None, 'rows', 'grp'), may hold values from -6 to 6
- diag_inverse: bfloat16 [3, 128, 4, 512, 512], P(None, 'rows', 'grp'), as said below
- coupling: bfloat16 [3, 128, 4, 512, 512], P(None, 'rows', 'grp'), may hold values from -0.125 to 0.125
- off_block: bfloat16 [2, 128, 4, 512, 512], P(None, 'rows', 'grp'), may hold values from -0.1875 to 0.1875
- off_route: int32 [2, 128, 4], P(None, 'rows', 'grp'), may hold values from 0 to 255, as said below
Outputs:
- solution: float32 [3, 128, 4, 2, 512], P(None, 'rows', 'grp')
The draws below stay inside these ranges and needn't reach their ends.
Inputs may be any that keep to these rules, and one draw needn't show every extreme that they name: `off_route`: for a block of super-level l the value is s * 128 + t with 0 <= s <= 1 - l: the block belongs to block row t of the same group in super-level l + 1 + s. `diag_inverse`: each matrix is a dominant diagonal plus independent off-diagonal entries.
All inputs are finite; a program needn't handle non-finite values.
Results may differ from the reference program's by a relative error of at most 0.0045.
Values may be sent and summed in bfloat16 or wider, within the bound.
A program may use at most 64 MiB of HBM per device.

```python
import math
import jax
import jax.numpy as jnp
from jax import lax

B = 512
NRHS = 2
LEVELS = 3
ROWBLOCKS = 128
GROUPS = 4


def draw_diag_inverse(key, part):
    dims_shape = (LEVELS, ROWBLOCKS, GROUPS, B, B)
    first_key, second_key = jax.random.split(jax.random.fold_in(key, 11))
    diagonal = jax.random.uniform(first_key, dims_shape[:4], jnp.float32, 0.5, 1.5)
    random_part = 0.6 / math.sqrt(B) * jax.random.normal(second_key, dims_shape, jnp.float32)
    identity_matrix = jnp.eye(B, dtype=jnp.float32)
    return (random_part + diagonal[..., None] * identity_matrix).astype(jnp.bfloat16)


def draw_off_route(key, part):
    dims_shape = (LEVELS - 1, ROWBLOCKS, GROUPS)
    first_key, second_key = jax.random.split(jax.random.fold_in(key, 23))
    ahead_limit = LEVELS - 1 - jnp.arange(LEVELS - 1, dtype=jnp.int32)
    level_skip = jax.random.randint(first_key, dims_shape, 0, 1 << 20, dtype=jnp.int32) % ahead_limit[:, None, None]
    target_row = jax.random.randint(second_key, dims_shape, 0, ROWBLOCKS, dtype=jnp.int32)
    return (level_skip * ROWBLOCKS + target_row).astype(jnp.int32)


def steps_of(own_key, extent, cuts, smallest, largest):
    def one(dim, blocks):
        heights = jax.random.uniform(jax.random.fold_in(jax.random.fold_in(own_key, 6), dim), (blocks,), jnp.float32, smallest / len(cuts), largest / len(cuts))
        return jnp.repeat(jnp.exp(heights), extent[dim] // blocks).reshape((-1,) + (1,) * (len(extent) - dim - 1))

    level = one(*cuts[0])
    for cut in cuts[1:]:
        level = level * one(*cut)
    return level


def bell_draw(stream_key, dims, deviation, most, cuts=(), held_as=jnp.bfloat16):
    factor_of = steps_of(stream_key, dims, cuts, -0.22, 0.18) if cuts else 1.0
    array = jax.random.normal(stream_key, dims, jnp.float32) * deviation * factor_of
    return jnp.minimum(jnp.maximum(array, -most), most).astype(held_as)


def setup_inputs(seed: int = 0) -> dict:
    key_of = jax.random.split(jax.random.key(seed), 6)
    rhs = bell_draw(key_of[0], (LEVELS, ROWBLOCKS, GROUPS, NRHS, B), 1.0, 6.0, ((1, 128), (2, 4)), jnp.float32)
    diag_inverse = draw_diag_inverse(jax.random.fold_in(key_of[5], 71), 0)
    coupling = bell_draw(key_of[2], (LEVELS, ROWBLOCKS, GROUPS, B, B), (4 * B) ** -0.5, 0.125, ((1, 128), (2, 4)))
    off_block = bell_draw(key_of[3], (LEVELS - 1, ROWBLOCKS, GROUPS, B, B), (2 * B) ** -0.5, 0.1875, ((1, 128), (2, 4)))
    off_route = draw_off_route(jax.random.fold_in(key_of[5], 71), 0)
    return dict(rhs=rhs, diag_inverse=diag_inverse, coupling=coupling, off_block=off_block, off_route=off_route)


def reference(rhs, diag_inverse, coupling, off_block, off_route):
    highest = lax.Precision.HIGHEST
    incoming = jnp.zeros(rhs.shape, jnp.float32)
    group_index = jnp.arange(GROUPS, dtype=jnp.int32)[None, :]
    results = []
    for super_level in range(LEVELS):
        source = rhs[super_level] - incoming[super_level]
        inverse = diag_inverse[super_level]
        coupler = coupling[super_level]
        columns = []
        previous = None
        for group_number in range(GROUPS):
            partial_rhs = source[:, group_number]
            if previous is not None:
                partial_rhs = partial_rhs - jnp.einsum("rkb,rbc->rkc", previous, coupler[:, group_number].astype(jnp.float32), precision=highest)
            previous = jnp.einsum("rkb,rbc->rkc", partial_rhs, inverse[:, group_number].astype(jnp.float32), precision=highest)
            columns.append(previous)
        solved = jnp.stack(columns, axis=1)
        results.append(solved)
        if super_level < LEVELS - 1:
            rounded = lax.optimization_barrier(solved.astype(jnp.bfloat16)).astype(jnp.float32)
            contribution = jnp.einsum("rgkb,rgbc->rgkc", rounded, off_block[super_level].astype(jnp.float32), precision=highest)
            contribution = lax.optimization_barrier(contribution.astype(jnp.bfloat16)).astype(jnp.float32)
            routing = off_route[super_level]
            level_skip = routing // ROWBLOCKS
            target_row = routing % ROWBLOCKS
            incoming = incoming.at[super_level + 1 + level_skip, target_row, group_index].add(contribution)
    return jnp.stack(results, axis=0)
```

```python
import functools

import jax
import jax.numpy as jnp
from jax import lax
from jax.experimental import pallas as pl
from jax.experimental.pallas import tpu as pltpu
from jax.sharding import PartitionSpec as P

INNER = 8
MESH = pl.DeviceIdType.MESH


def far_first(count):
    return sorted(range(1, count), key=lambda offset: -min(offset, count - offset))


def kernel(
    outer, groups, rhs_hbm, inverse_hbm, coupler_hbm, block_hbm, route_hbm, out_ref,
    rhs, inverse, coupler, block, route, code, codes, solved, before, sent, zland, held, part, yland,
    in_sem, code_send, code_recv, x_send, x_recv, z_send, z_recv, y_send, y_recv,
):
    levels = rhs.shape[0]
    rowblocks = outer * INNER
    row = lax.axis_index("rows")
    grp = lax.axis_index("grp")
    zpos = row // INNER
    spot = row % INNER

    def z_peer(offset):
        return {"rows": ((zpos + offset) % outer) * INNER + spot}

    def y_peer(offset):
        return {"rows": zpos * INNER + (spot + offset) % INNER}

    barrier = pltpu.get_barrier_semaphore()
    for offset in far_first(outer):
        pl.semaphore_signal(barrier, inc=1, device_id=z_peer(offset), device_id_type=MESH)
    for offset in far_first(INNER):
        pl.semaphore_signal(barrier, inc=1, device_id=y_peer(offset), device_id_type=MESH)

    left = {"grp": (grp + groups - 1) % groups}
    pl.semaphore_signal(barrier, inc=1, device_id=left, device_id_type=MESH)

    loads = [pltpu.make_async_copy(rhs_hbm, rhs, in_sem.at[0]), pltpu.make_async_copy(route_hbm, route, in_sem.at[1])]
    index = 2
    matrices = []
    for level in range(levels):
        entry = {}
        for name, source, target in (("D", inverse_hbm, inverse), ("E", block_hbm, block), ("C", coupler_hbm, coupler)):
            if name == "E" and level == levels - 1:
                continue
            copy = pltpu.make_async_copy(source.at[level], target.at[level], in_sem.at[index])
            index += 1
            loads.append(copy)
            entry[name] = copy
        matrices.append(entry)
    for copy in loads:
        copy.start()

    quarter = lax.broadcasted_iota(jnp.int32, (8, 128), 0) // 2

    def spread(v8):
        return jnp.concatenate([jnp.where(quarter == j, v8, 0.0) for j in range(4)], axis=1)

    def fold(p):
        q = p + pltpu.roll(p, 4, 0)
        q = q + pltpu.roll(q, 2, 0)
        out = q[:, 0:128]
        for j in range(1, 4):
            out = jnp.where(quarter == j, q[:, 128 * j : 128 * (j + 1)], out)
        return out

    def product(v8, matrix):
        wide = spread(v8)
        low = wide - wide.astype(jnp.bfloat16).astype(jnp.float32)
        stack = jnp.concatenate([wide, low], axis=0).astype(jnp.bfloat16)
        p = jnp.dot(stack, matrix, preferred_element_type=jnp.float32)
        return fold(p[0:8] + p[8:16])

    def rounded_product(v8, matrix):
        wide = spread(v8)
        stack = jnp.concatenate([wide, jnp.zeros_like(wide)], axis=0).astype(jnp.bfloat16)
        p = jnp.dot(stack, matrix, preferred_element_type=jnp.float32)
        return fold(p[0:8])

    def contribute(level):
        sent[level] = rounded_product(solved[level], block[level]).astype(jnp.bfloat16)

    loads[0].wait()
    loads[1].wait()
    both = route[0, 0] + 256 * route[0, 1]
    code[...] = jnp.full((1, 128), both, jnp.int32)
    matrices[0]["D"].wait()
    solved[0] = product(rhs[0], inverse[0])
    matrices[0]["E"].wait()
    contribute(0)
    matrices[0]["C"].wait()

    pl.semaphore_wait(barrier, outer - 1 + INNER - 1 + 1)

    def code_copy(offset):
        return pltpu.make_async_remote_copy(
            src_ref=code, dst_ref=codes.at[offset], send_sem=code_send, recv_sem=code_recv,
            device_id=z_peer(offset), device_id_type=MESH,
        )

    def x_copy(level):
        return pltpu.make_async_remote_copy(
            src_ref=solved.at[level], dst_ref=before.at[level], send_sem=x_send.at[level], recv_sem=x_recv.at[level],
            device_id={"grp": grp + 1}, device_id_type=MESH,
        )

    def z_copy(level, offset):
        return pltpu.make_async_remote_copy(
            src_ref=sent.at[level], dst_ref=zland.at[level, offset], send_sem=z_send.at[level], recv_sem=z_recv.at[level],
            device_id=z_peer(offset), device_id_type=MESH,
        )

    def y_copy(level, offset):
        return pltpu.make_async_remote_copy(
            src_ref=part.at[level, offset], dst_ref=yland.at[level, offset], send_sem=y_send.at[level],
            recv_sem=y_recv.at[level], device_id=y_peer(offset), device_id_type=MESH,
        )

    def bulk_wait(ref, sem):
        pltpu.make_async_copy(ref, ref, sem).wait()

    z_order, y_order = far_first(outer), far_first(INNER)

    for level in range(levels):
        if level > 0:
            matrices[level]["D"].wait()
            matrices[level]["C"].wait()
            if level < levels - 1:
                matrices[level]["E"].wait()
            bulk_wait(yland.at[level - 1, pl.ds(1, INNER - 1)], y_recv.at[level - 1])
            incoming = part[level - 1, 0]
            for offset in range(1, INNER):
                incoming = incoming + yland[level - 1, offset]
            solved[level] = product(rhs[level] - incoming, inverse[level])

        @pl.when(grp > 0)
        def _():
            bulk_wait(before.at[level], x_recv.at[level])
            solved[level] = solved[level] - product(product(before[level], coupler[level]), inverse[level])

        @pl.when(grp < groups - 1)
        def _():
            x_copy(level).start()

        if level == levels - 1:
            break
        if level == 0:
            @pl.when(grp > 0)
            def _():
                contribute(0)
        else:
            contribute(level)
        for offset in z_order:
            z_copy(level, offset).start()
        if level == 0:
            for offset in z_order:
                code_copy(offset).start()
            codes[0] = code[...]
            bulk_wait(codes.at[pl.ds(1, outer - 1)], code_recv)
        bulk_wait(zland.at[level, pl.ds(1, outer - 1)], z_recv.at[level])

        arrived = [sent[level].astype(jnp.float32)]
        arrived += [zland[level, offset].astype(jnp.float32) for offset in range(1, outer)]
        marks = [jnp.broadcast_to(codes[offset], (8, 128)) for offset in range(outer)]
        marks = [(mark // 256 if level else mark % 256) for mark in marks]

        def gathered(target):
            terms = [jnp.where(mark == target, value, 0.0) for mark, value in zip(marks, arrived)]
            while len(terms) > 1:
                terms = [terms[i] + terms[i + 1] for i in range(0, len(terms), 2)]
            return terms[0]

        for offset in y_order + [0]:
            target = zpos * INNER + (spot + offset) % INNER
            total = gathered(target)
            if level > 0:
                total = total + held[offset]
            part[level, offset] = total
            if offset:
                y_copy(level, offset).start()
        if level == 0:
            for offset in range(INNER):
                held[offset] = gathered(zpos * INNER + (spot + offset) % INNER + rowblocks)

    out_ref[...] = solved[...]

    bulk_wait(codes.at[pl.ds(1, outer - 1)], code_send)
    for level in range(levels - 1):
        bulk_wait(zland.at[level, pl.ds(1, outer - 1)], z_send.at[level])
        bulk_wait(part.at[level, pl.ds(1, INNER - 1)], y_send.at[level])

    @pl.when(grp < groups - 1)
    def _():
        for level in range(levels):
            bulk_wait(solved.at[level], x_send.at[level])


def shards(rhs, diag_inverse, coupling, off_block, off_route):
    groups = lax.axis_size("grp")
    outer = lax.axis_size("rows") // INNER
    levels, size = rhs.shape[0], rhs.shape[-1]
    assert levels == 3 and rhs.shape[-2:] == (2, 512)
    rows8 = rhs[:, 0, 0].reshape(levels, 2, 4, 128).transpose(0, 2, 1, 3).reshape(levels, 8, 128)
    hbm = pl.BlockSpec(memory_space=pl.ANY)
    dma = pltpu.SemaphoreType.DMA
    out = pl.pallas_call(
        functools.partial(kernel, outer, groups),
        out_shape=jax.ShapeDtypeStruct((levels, 8, 128), jnp.float32),
        in_specs=[hbm] * 5,
        out_specs=pl.BlockSpec(memory_space=pltpu.VMEM),
        scratch_shapes=[
            pltpu.VMEM((levels, 8, 128), jnp.float32),
            pltpu.VMEM((levels, size, size), jnp.bfloat16),
            pltpu.VMEM((levels, size, size), jnp.bfloat16),
            pltpu.VMEM((levels - 1, size, size), jnp.bfloat16),
            pltpu.SMEM((1, levels - 1), jnp.int32),
            pltpu.VMEM((1, 128), jnp.int32),
            pltpu.VMEM((outer, 1, 128), jnp.int32),
            pltpu.VMEM((levels, 8, 128), jnp.float32),
            pltpu.VMEM((levels, 8, 128), jnp.float32),
            pltpu.VMEM((levels - 1, 8, 128), jnp.bfloat16),
            pltpu.VMEM((levels - 1, outer, 8, 128), jnp.bfloat16),
            pltpu.VMEM((INNER, 8, 128), jnp.float32),
            pltpu.VMEM((levels - 1, INNER, 8, 128), jnp.float32),
            pltpu.VMEM((levels - 1, INNER, 8, 128), jnp.float32),
            dma((2 + 3 * levels - 1,)),
            dma, dma,
            dma((levels,)), dma((levels,)),
            dma((levels - 1,)), dma((levels - 1,)),
            dma((levels - 1,)), dma((levels - 1,)),
        ],
        compiler_params=pltpu.CompilerParams(collective_id=0, has_side_effects=True),
    )(rows8, diag_inverse[:, 0, 0], coupling[:, 0, 0], off_block[:, 0, 0], off_route[:, 0].T)
    out = out.reshape(levels, 4, 2, 128).transpose(0, 2, 1, 3).reshape(levels, 2, size)
    return out[:, None, None]


def solution(mesh):
    return jax.shard_map(
        shards,
        mesh=mesh,
        in_specs=(
            P(None, "rows", "grp", None, None),
            P(None, "rows", "grp", None, None),
            P(None, "rows", "grp", None, None),
            P(None, "rows", "grp", None, None),
            P(None, "rows", "grp"),
        ),
        out_specs=P(None, "rows", "grp", None, None),
        check_vma=False,
    )
```

```python
import functools

import jax
import jax.numpy as jnp
from jax import lax
from jax.experimental import pallas as pl
from jax.experimental.pallas import tpu as pltpu
from jax.sharding import PartitionSpec as P

INNER = 8
MESH = pl.DeviceIdType.MESH


def far_first(count):
    return sorted(range(1, count), key=lambda offset: -min(offset, count - offset))


def kernel(
    outer, groups, rhs_hbm, inverse_hbm, coupler_hbm, block_hbm, route_hbm, out_ref,
    rhs, inverse, coupler, block, route, code, codes, solved, before, sent, yland, held, part, zland,
    in_sem, meet, code_send, code_recv, x_send, x_recv, y_send, y_recv, z_send, z_recv,
):
    levels = rhs.shape[0]
    rowblocks = outer * INNER
    row = lax.axis_index("rows")
    grp = lax.axis_index("grp")
    zpos = row // INNER
    spot = row % INNER

    def z_peer(offset):
        return {"rows": ((zpos + offset) % outer) * INNER + spot}

    def y_peer(offset):
        return {"rows": zpos * INNER + (spot + offset) % INNER}

    barrier = pltpu.get_barrier_semaphore()
    for offset in (1, outer - 1):
        pl.semaphore_signal(barrier, inc=1, device_id=z_peer(offset), device_id_type=MESH)
    for offset in far_first(INNER):
        pl.semaphore_signal(barrier, inc=1, device_id=y_peer(offset), device_id_type=MESH)
    left = {"grp": (grp + groups - 1) % groups}
    pl.semaphore_signal(barrier, inc=1, device_id=left, device_id_type=MESH)

    loads = [pltpu.make_async_copy(rhs_hbm, rhs, in_sem.at[0]), pltpu.make_async_copy(route_hbm, route, in_sem.at[1])]
    index = 2
    matrices = []
    for level in range(levels):
        entry = {}
        for name, source, target in (("D", inverse_hbm, inverse), ("E", block_hbm, block), ("C", coupler_hbm, coupler)):
            if name == "E" and level == levels - 1:
                continue
            copy = pltpu.make_async_copy(source.at[level], target.at[level], in_sem.at[index])
            index += 1
            loads.append(copy)
            entry[name] = copy
        matrices.append(entry)
    first = loads[:5]
    for copy in first:
        copy.start()

    quarter = lax.broadcasted_iota(jnp.int32, (8, 128), 0) // 2

    def spread(v8):
        return jnp.concatenate([jnp.where(quarter == j, v8, 0.0) for j in range(4)], axis=1)

    def fold(p):
        q = p + pltpu.roll(p, 4, 0)
        q = q + pltpu.roll(q, 2, 0)
        out = q[:, 0:128]
        for j in range(1, 4):
            out = jnp.where(quarter == j, q[:, 128 * j : 128 * (j + 1)], out)
        return out

    def product(v8, matrix):
        wide = spread(v8)
        low = wide - wide.astype(jnp.bfloat16).astype(jnp.float32)
        stack = jnp.concatenate([wide, low], axis=0).astype(jnp.bfloat16)
        p = jnp.dot(stack, matrix, preferred_element_type=jnp.float32)
        return fold(p[0:8] + p[8:16])

    def rounded_product(v8, matrix):
        wide = spread(v8)
        stack = jnp.concatenate([wide, jnp.zeros_like(wide)], axis=0).astype(jnp.bfloat16)
        p = jnp.dot(stack, matrix, preferred_element_type=jnp.float32)
        return fold(p[0:8])

    def contribute(level):
        sent[level] = rounded_product(solved[level], block[level]).astype(jnp.bfloat16)

    loads[0].wait()
    loads[1].wait()
    both = route[0, 0] + 256 * route[0, 1]
    code[...] = jnp.full((1, 128), both, jnp.int32)
    matrices[0]["D"].wait()
    for copy in loads[5:]:
        copy.start()
    solved[0] = product(rhs[0], inverse[0])
    matrices[0]["E"].wait()
    contribute(0)
    matrices[0]["C"].wait()

    pl.semaphore_wait(barrier, 2 + INNER - 1 + 1)

    rounds = max(1, (outer // 2 - 1).bit_length())

    def greet(step):
        for offset in (2**step, outer - 2**step):
            pl.semaphore_signal(meet.at[step], inc=1, device_id=z_peer(offset), device_id_type=MESH)

    def met(step):
        pl.semaphore_wait(meet.at[step], 2)

    greet(0)

    def code_copy(offset):
        return pltpu.make_async_remote_copy(
            src_ref=code, dst_ref=codes.at[offset], send_sem=code_send, recv_sem=code_recv,
            device_id=y_peer(offset), device_id_type=MESH,
        )

    def x_copy(level):
        return pltpu.make_async_remote_copy(
            src_ref=solved.at[level], dst_ref=before.at[level], send_sem=x_send.at[level], recv_sem=x_recv.at[level],
            device_id={"grp": grp + 1}, device_id_type=MESH,
        )

    def y_copy(level, offset):
        return pltpu.make_async_remote_copy(
            src_ref=sent.at[level], dst_ref=yland.at[level, offset], send_sem=y_send.at[level],
            recv_sem=y_recv.at[level], device_id=y_peer(offset), device_id_type=MESH,
        )

    def z_copy(level, offset):
        return pltpu.make_async_remote_copy(
            src_ref=part.at[level, offset], dst_ref=zland.at[level, offset], send_sem=z_send.at[level],
            recv_sem=z_recv.at[level], device_id=z_peer(offset), device_id_type=MESH,
        )

    def bulk_wait(ref, sem):
        pltpu.make_async_copy(ref, ref, sem).wait()

    z_order, y_order = far_first(outer), far_first(INNER)

    def scatter(level):
        for offset in y_order:
            y_copy(level, offset).start()

    for offset in y_order:
        code_copy(offset).start()
    codes[0] = code[...]

    def total_of(terms):
        while len(terms) > 1:
            terms = [terms[i] + terms[i + 1] for i in range(0, len(terms) - 1, 2)] + terms[len(terms) & ~1 :]
        return terms[0]

    for level in range(levels):
        if level > 0:
            matrices[level]["D"].wait()
            matrices[level]["C"].wait()
            if level < levels - 1:
                matrices[level]["E"].wait()
            bulk_wait(zland.at[level - 1, pl.ds(1, outer - 1)], z_recv.at[level - 1])
            incoming = total_of(
                [part[level - 1, 0].astype(jnp.float32)]
                + [zland[level - 1, offset].astype(jnp.float32) for offset in range(1, outer)]
            )
            solved[level] = product(rhs[level] - incoming, inverse[level])
        else:
            @pl.when(grp == 0)
            def _():
                x_copy(0).start()
                scatter(0)

            met(0)
            if rounds > 1:
                greet(1)

        @pl.when(grp > 0)
        def _():
            bulk_wait(before.at[level], x_recv.at[level])
            solved[level] = solved[level] - product(product(before[level], coupler[level]), inverse[level])

            @pl.when(grp < groups - 1)
            def _():
                x_copy(level).start()

            if level == 0:
                contribute(0)
                scatter(0)

        if level > 0:
            @pl.when(grp == 0)
            def _():
                x_copy(level).start()

        if level == levels - 1:
            break
        if level > 0:
            contribute(level)
            scatter(level)
        else:
            for step in range(1, rounds):
                met(step)
                if step + 1 < rounds:
                    greet(step + 1)
            bulk_wait(codes.at[pl.ds(1, INNER - 1)], code_recv)
        bulk_wait(yland.at[level, pl.ds(1, INNER - 1)], y_recv.at[level])

        arrived = [sent[level].astype(jnp.float32)]
        arrived += [yland[level, offset].astype(jnp.float32) for offset in range(1, INNER)]
        marks = [jnp.broadcast_to(codes[offset], (8, 128)) for offset in range(INNER)]
        marks = [(mark // 256 if level else mark % 256) for mark in marks]

        def gathered(target):
            return total_of([jnp.where(mark == target, value, 0.0) for mark, value in zip(marks, arrived)])

        for offset in z_order + [0]:
            target = ((zpos + offset) % outer) * INNER + spot
            total = gathered(target)
            if level > 0:
                total = total + held[offset]
            part[level, offset] = total.astype(jnp.bfloat16)
            if offset:
                z_copy(level, offset).start()
        if level == 0:
            for offset in range(outer):
                held[offset] = gathered(((zpos + offset) % outer) * INNER + spot + rowblocks)

    out_ref[...] = solved[...]

    bulk_wait(codes.at[pl.ds(1, INNER - 1)], code_send)
    for level in range(levels - 1):
        bulk_wait(yland.at[level, pl.ds(1, INNER - 1)], y_send.at[level])
        bulk_wait(zland.at[level, pl.ds(1, outer - 1)], z_send.at[level])

    @pl.when(grp < groups - 1)
    def _():
        for level in range(levels):
            bulk_wait(solved.at[level], x_send.at[level])


def shards(rhs, diag_inverse, coupling, off_block, off_route):
    groups = lax.axis_size("grp")
    outer = lax.axis_size("rows") // INNER
    levels, size = rhs.shape[0], rhs.shape[-1]
    assert levels == 3 and rhs.shape[-2:] == (2, 512)
    rows8 = rhs[:, 0, 0].reshape(levels, 2, 4, 128).transpose(0, 2, 1, 3).reshape(levels, 8, 128)
    hbm = pl.BlockSpec(memory_space=pl.ANY)
    dma = pltpu.SemaphoreType.DMA
    out = pl.pallas_call(
        functools.partial(kernel, outer, groups),
        out_shape=pltpu.VMEM((levels, 8, 128), jnp.float32),
        in_specs=[hbm] * 5,
        out_specs=pl.BlockSpec(memory_space=pltpu.VMEM),
        scratch_shapes=[
            pltpu.VMEM((levels, 8, 128), jnp.float32),
            pltpu.VMEM((levels, size, size), jnp.bfloat16),
            pltpu.VMEM((levels, size, size), jnp.bfloat16),
            pltpu.VMEM((levels - 1, size, size), jnp.bfloat16),
            pltpu.SMEM((1, levels - 1), jnp.int32),
            pltpu.VMEM((1, 128), jnp.int32),
            pltpu.VMEM((INNER, 1, 128), jnp.int32),
            pltpu.VMEM((levels, 8, 128), jnp.float32),
            pltpu.VMEM((levels, 8, 128), jnp.float32),
            pltpu.VMEM((levels - 1, 8, 128), jnp.bfloat16),
            pltpu.VMEM((levels - 1, INNER, 8, 128), jnp.bfloat16),
            pltpu.VMEM((outer, 8, 128), jnp.float32),
            pltpu.VMEM((levels - 1, outer, 8, 128), jnp.bfloat16),
            pltpu.VMEM((levels - 1, outer, 8, 128), jnp.bfloat16),
            dma((2 + 3 * levels - 1,)),
            pltpu.SemaphoreType.REGULAR((max(1, (outer // 2 - 1).bit_length()),)),
            dma, dma,
            dma((levels,)), dma((levels,)),
            dma((levels - 1,)), dma((levels - 1,)),
            dma((levels - 1,)), dma((levels - 1,)),
        ],
        compiler_params=pltpu.CompilerParams(collective_id=0, has_side_effects=True),
    )(rows8, diag_inverse[:, 0, 0], coupling[:, 0, 0], off_block[:, 0, 0], off_route[:, 0].T)
    out = out.reshape(levels, 4, 2, 128).transpose(0, 2, 1, 3).reshape(levels, 2, size)
    return out[:, None, None]


def solution(mesh):
    return jax.shard_map(
        shards,
        mesh=mesh,
        in_specs=(
            P(None, "rows", "grp", None, None),
            P(None, "rows", "grp", None, None),
            P(None, "rows", "grp", None, None),
            P(None, "rows", "grp", None, None),
            P(None, "rows", "grp"),
        ),
        out_specs=P(None, "rows", "grp", None, None),
        check_vma=False,
    )
```

```python
import functools

import jax
import jax.numpy as jnp
from jax import lax
from jax.experimental import pallas as pl
from jax.experimental.pallas import tpu as pltpu
from jax.sharding import PartitionSpec as P

INNER = 8
MESH = pl.DeviceIdType.MESH


def far_first(count):
    return sorted(range(1, count), key=lambda offset: -min(offset, count - offset))


def kernel(
    outer, groups, rhs_hbm, inverse_hbm, coupler_hbm, block_hbm, route_hbm, out_ref,
    rhs, inverse, coupler, block, route, code, codes, solved, before, sent, early, relay, direct, yland, held, part, zland,
    in_sem, meet, code_send, code_recv, x_send, x_recv, y_send, y_recv, z_send, z_recv,
):
    levels = rhs.shape[0]
    rowblocks = outer * INNER
    row = lax.axis_index("rows")
    grp = lax.axis_index("grp")
    zpos = row // INNER
    spot = row % INNER

    def z_peer(offset):
        return {"rows": ((zpos + offset) % outer) * INNER + spot}

    def y_peer(offset):
        return {"rows": zpos * INNER + (spot + offset) % INNER}

    barrier = pltpu.get_barrier_semaphore()
    near = sorted({offset % outer for offset in (2, -2, 1, -1)} - {0})
    for offset in near:
        pl.semaphore_signal(barrier, inc=1, device_id=z_peer(offset), device_id_type=MESH)
    for offset in far_first(INNER):
        pl.semaphore_signal(barrier, inc=1, device_id=y_peer(offset), device_id_type=MESH)
    left = {"grp": (grp + groups - 1) % groups}
    pl.semaphore_signal(barrier, inc=1, device_id=left, device_id_type=MESH)

    loads = [pltpu.make_async_copy(rhs_hbm, rhs, in_sem.at[0]), pltpu.make_async_copy(route_hbm, route, in_sem.at[1])]
    index = 2
    matrices = []
    for level in range(levels):
        entry = {}
        for name, source, target in (("D", inverse_hbm, inverse), ("E", block_hbm, block), ("C", coupler_hbm, coupler)):
            if name == "E" and level == levels - 1:
                continue
            copy = pltpu.make_async_copy(source.at[level], target.at[level], in_sem.at[index])
            index += 1
            loads.append(copy)
            entry[name] = copy
        matrices.append(entry)
    first = loads[:5]
    for copy in first:
        copy.start()

    quarter = lax.broadcasted_iota(jnp.int32, (8, 128), 0) // 2

    def spread(v8):
        return jnp.concatenate([jnp.where(quarter == j, v8, 0.0) for j in range(4)], axis=1)

    def fold(p):
        q = p + pltpu.roll(p, 4, 0)
        q = q + pltpu.roll(q, 2, 0)
        out = q[:, 0:128]
        for j in range(1, 4):
            out = jnp.where(quarter == j, q[:, 128 * j : 128 * (j + 1)], out)
        return out

    def product(v8, matrix):
        wide = spread(v8)
        low = wide - wide.astype(jnp.bfloat16).astype(jnp.float32)
        stack = jnp.concatenate([wide, low], axis=0).astype(jnp.bfloat16)
        p = jnp.dot(stack, matrix, preferred_element_type=jnp.float32)
        return fold(p[0:8] + p[8:16])

    def rounded_product(v8, matrix):
        wide = spread(v8)
        stack = jnp.concatenate([wide, jnp.zeros_like(wide)], axis=0).astype(jnp.bfloat16)
        p = jnp.dot(stack, matrix, preferred_element_type=jnp.float32)
        return fold(p[0:8])

    def contribution(level):
        return rounded_product(solved[level], block[level])

    def combine(level):
        def half(step, carry):
            rows = pl.ds(pl.multiple_of(step * 256, 256), 256)
            both = jnp.dot(coupler[level, rows], inverse[level], preferred_element_type=jnp.float32)
            relay[level, rows] = both.astype(jnp.bfloat16)
            if level < levels - 1:
                onward = jnp.dot(relay[level, rows], block[level], preferred_element_type=jnp.float32)
                direct[level, rows] = onward.astype(jnp.bfloat16)
            return carry

        lax.fori_loop(0, 2, half, 0)

    strides, known = [], min(2, outer // 2)
    while known < outer // 2:
        strides.append(min(known, outer // 2 - known))
        known += strides[-1]

    def greet(step):
        for offset in sorted({strides[step], outer - strides[step]}):
            pl.semaphore_signal(meet.at[step], inc=1, device_id=z_peer(offset), device_id_type=MESH)

    def met(step):
        pl.semaphore_wait(meet.at[step], len({strides[step], outer - strides[step]}))

    pl.semaphore_wait(barrier, len(near) + INNER - 1 + 1)
    if strides:
        greet(0)

    def code_copy(offset):
        return pltpu.make_async_remote_copy(
            src_ref=code, dst_ref=codes.at[offset], send_sem=code_send, recv_sem=code_recv,
            device_id=y_peer(offset), device_id_type=MESH,
        )

    def x_copy(level):
        return pltpu.make_async_remote_copy(
            src_ref=solved.at[level], dst_ref=before.at[level], send_sem=x_send.at[level], recv_sem=x_recv.at[level],
            device_id={"grp": grp + 1}, device_id_type=MESH,
        )

    def y_copy(level, offset):
        return pltpu.make_async_remote_copy(
            src_ref=sent.at[level], dst_ref=yland.at[level, offset], send_sem=y_send.at[level],
            recv_sem=y_recv.at[level], device_id=y_peer(offset), device_id_type=MESH,
        )

    def z_copy(level, offset):
        return pltpu.make_async_remote_copy(
            src_ref=part.at[level, offset], dst_ref=zland.at[level, offset], send_sem=z_send.at[level],
            recv_sem=z_recv.at[level], device_id=z_peer(offset), device_id_type=MESH,
        )

    def bulk_wait(ref, sem):
        pltpu.make_async_copy(ref, ref, sem).wait()

    z_order, y_order = far_first(outer), far_first(INNER)

    def scatter(level):
        for offset in y_order:
            y_copy(level, offset).start()

    def total_of(terms):
        while len(terms) > 1:
            terms = [terms[i] + terms[i + 1] for i in range(0, len(terms) - 1, 2)] + terms[len(terms) & ~1 :]
        return terms[0]

    loads[0].wait()
    matrices[0]["D"].wait()
    for copy in loads[5:]:
        copy.start()
    solved[0] = product(rhs[0], inverse[0])

    @pl.when(grp == 0)
    def _():
        x_copy(0).start()

    matrices[0]["E"].wait()
    early[0] = contribution(0)
    loads[1].wait()
    both = route[0, 0] + 256 * route[0, 1]
    code[...] = jnp.full((1, 128), both, jnp.int32)
    codes[0] = code[...]

    @pl.when(grp == 0)
    def _():
        sent[0] = early[0].astype(jnp.bfloat16)
        scatter(0)

    for offset in y_order:
        code_copy(offset).start()
    if strides:
        met(0)
        for step in range(1, len(strides)):
            greet(step)
            if step < len(strides) - 1:
                met(step)
    matrices[0]["C"].wait()

    @pl.when(grp > 0)
    def _():
        combine(0)

    for level in range(levels):
        last = level == levels - 1
        if level > 0:
            bulk_wait(zland.at[level - 1, pl.ds(1, outer - 1)], z_recv.at[level - 1])
            incoming = total_of(
                [part[level - 1, 0].astype(jnp.float32)]
                + [zland[level - 1, offset].astype(jnp.float32) for offset in range(1, outer)]
            )
            solved[level] = product(rhs[level] - incoming, inverse[level])

            @pl.when(grp == 0)
            def _():
                x_copy(level).start()
                if not last:
                    sent[level] = contribution(level).astype(jnp.bfloat16)
                    scatter(level)

            if not last:
                @pl.when(grp > 0)
                def _():
                    early[level] = contribution(level)

        @pl.when(grp > 0)
        def _():
            bulk_wait(before.at[level], x_recv.at[level])
            prior = before[level]
            solved[level] = solved[level] - product(prior, relay[level])

            @pl.when(grp < groups - 1)
            def _():
                x_copy(level).start()

            if not last:
                sent[level] = (early[level] - product(prior, direct[level])).astype(jnp.bfloat16)
                scatter(level)

        if last:
            break
        if level == 0:
            bulk_wait(codes.at[pl.ds(1, INNER - 1)], code_recv)
        bulk_wait(yland.at[level, pl.ds(1, INNER - 1)], y_recv.at[level])

        arrived = [sent[level].astype(jnp.float32)]
        arrived += [yland[level, offset].astype(jnp.float32) for offset in range(1, INNER)]
        marks = [jnp.broadcast_to(codes[offset], (8, 128)) for offset in range(INNER)]
        marks = [(mark // 256 if level else mark % 256) for mark in marks]

        def gathered(target):
            return total_of([jnp.where(mark == target, value, 0.0) for mark, value in zip(marks, arrived)])

        for offset in z_order + [0]:
            target = ((zpos + offset) % outer) * INNER + spot
            total = gathered(target)
            if level > 0:
                total = total + held[offset]
            part[level, offset] = total.astype(jnp.bfloat16)
            if level == 0 and len(strides) > 1 and offset == z_order[0]:
                met(len(strides) - 1)
            if offset:
                z_copy(level, offset).start()
        if level == 0:
            for offset in range(outer):
                held[offset] = gathered(((zpos + offset) % outer) * INNER + spot + rowblocks)
            for copy in loads[5:]:
                copy.wait()

            @pl.when(grp > 0)
            def _():
                for later in range(1, levels):
                    combine(later)

    out_ref[...] = solved[...]

    bulk_wait(codes.at[pl.ds(1, INNER - 1)], code_send)
    for level in range(levels - 1):
        bulk_wait(yland.at[level, pl.ds(1, INNER - 1)], y_send.at[level])
        bulk_wait(zland.at[level, pl.ds(1, outer - 1)], z_send.at[level])

    @pl.when(grp < groups - 1)
    def _():
        for level in range(levels):
            bulk_wait(solved.at[level], x_send.at[level])


def shards(rhs, diag_inverse, coupling, off_block, off_route):
    groups = lax.axis_size("grp")
    outer = lax.axis_size("rows") // INNER
    levels, size = rhs.shape[0], rhs.shape[-1]
    assert levels == 3 and rhs.shape[-2:] == (2, 512)
    rows8 = rhs[:, 0, 0].reshape(levels, 2, 4, 128).transpose(0, 2, 1, 3).reshape(levels, 8, 128)
    hbm = pl.BlockSpec(memory_space=pl.ANY)
    dma = pltpu.SemaphoreType.DMA
    out = pl.pallas_call(
        functools.partial(kernel, outer, groups),
        out_shape=pltpu.VMEM((levels, 8, 128), jnp.float32),
        in_specs=[hbm] * 5,
        out_specs=pl.BlockSpec(memory_space=pltpu.VMEM),
        scratch_shapes=[
            pltpu.VMEM((levels, 8, 128), jnp.float32),
            pltpu.VMEM((levels, size, size), jnp.bfloat16),
            pltpu.VMEM((levels, size, size), jnp.bfloat16),
            pltpu.VMEM((levels - 1, size, size), jnp.bfloat16),
            pltpu.SMEM((1, levels - 1), jnp.int32),
            pltpu.VMEM((1, 128), jnp.int32),
            pltpu.VMEM((INNER, 1, 128), jnp.int32),
            pltpu.VMEM((levels, 8, 128), jnp.float32),
            pltpu.VMEM((levels, 8, 128), jnp.float32),
            pltpu.VMEM((levels - 1, 8, 128), jnp.bfloat16),
            pltpu.VMEM((levels - 1, 8, 128), jnp.float32),
            pltpu.VMEM((levels, size, size), jnp.bfloat16),
            pltpu.VMEM((levels - 1, size, size), jnp.bfloat16),
            pltpu.VMEM((levels - 1, INNER, 8, 128), jnp.bfloat16),
            pltpu.VMEM((outer, 8, 128), jnp.float32),
            pltpu.VMEM((levels - 1, outer, 8, 128), jnp.bfloat16),
            pltpu.VMEM((levels - 1, outer, 8, 128), jnp.bfloat16),
            dma((2 + 3 * levels - 1,)),
            pltpu.SemaphoreType.REGULAR((max(1, outer.bit_length() - 2),)),
            dma, dma,
            dma((levels,)), dma((levels,)),
            dma((levels - 1,)), dma((levels - 1,)),
            dma((levels - 1,)), dma((levels - 1,)),
        ],
        compiler_params=pltpu.CompilerParams(collective_id=0, has_side_effects=True),
    )(rows8, diag_inverse[:, 0, 0], coupling[:, 0, 0], off_block[:, 0, 0], off_route[:, 0].T)
    out = out.reshape(levels, 4, 2, 128).transpose(0, 2, 1, 3).reshape(levels, 2, size)
    return out[:, None, None]


def solution(mesh):
    return jax.shard_map(
        shards,
        mesh=mesh,
        in_specs=(
            P(None, "rows", "grp", None, None),
            P(None, "rows", "grp", None, None),
            P(None, "rows", "grp", None, None),
            P(None, "rows", "grp", None, None),
            P(None, "rows", "grp"),
        ),
        out_specs=P(None, "rows", "grp", None, None),
        check_vma=False,
    )
```

```python
import functools

import jax
import jax.numpy as jnp
from jax import lax
from jax.experimental import pallas as pl
from jax.experimental.pallas import tpu as pltpu
from jax.sharding import PartitionSpec as P

INNER = 8
MESH = pl.DeviceIdType.MESH


def far_first(count):
    return sorted(range(1, count), key=lambda offset: -min(offset, count - offset))


def kernel(
    outer, groups, rhs_hbm, inverse_hbm, coupler_hbm, block_hbm, route_hbm, out_ref,
    rhs, inverse, coupler, block, route, code, codes, solved, before, sent, early, relay, direct, yland, held, part, zland,
    in_sem, meet, code_send, code_recv, x_send, x_recv, y_send, y_recv, z_send, z_recv,
):
    levels = rhs.shape[0]
    rowblocks = outer * INNER
    row = lax.axis_index("rows")
    grp = lax.axis_index("grp")
    zpos = row // INNER
    spot = row % INNER

    def z_peer(offset):
        return {"rows": ((zpos + offset) % outer) * INNER + spot}

    def y_peer(offset):
        return {"rows": zpos * INNER + (spot + offset) % INNER}

    barrier = pltpu.get_barrier_semaphore()
    near = sorted({offset % outer for offset in (4, -4, 3, -3, 2, -2, 1, -1)} - {0}, key=lambda offset: -min(offset, outer - offset))
    for offset in near:
        pl.semaphore_signal(barrier, inc=1, device_id=z_peer(offset), device_id_type=MESH)
    for offset in far_first(INNER):
        pl.semaphore_signal(barrier, inc=1, device_id=y_peer(offset), device_id_type=MESH)
    left = {"grp": (grp + groups - 1) % groups}
    pl.semaphore_signal(barrier, inc=1, device_id=left, device_id_type=MESH)

    loads = [pltpu.make_async_copy(rhs_hbm, rhs, in_sem.at[0]), pltpu.make_async_copy(route_hbm, route, in_sem.at[1])]
    index = 2
    matrices = []
    for level in range(levels):
        entry = {}
        for name, source, target in (("D", inverse_hbm, inverse), ("E", block_hbm, block), ("C", coupler_hbm, coupler)):
            if name == "E" and level == levels - 1:
                continue
            copy = pltpu.make_async_copy(source.at[level], target.at[level], in_sem.at[index])
            index += 1
            loads.append(copy)
            entry[name] = copy
        matrices.append(entry)
    first = loads[:5]
    for copy in first:
        copy.start()

    quarter = lax.broadcasted_iota(jnp.int32, (8, 128), 0) // 2

    def spread(v8):
        return jnp.concatenate([jnp.where(quarter == j, v8, 0.0) for j in range(4)], axis=1)

    def fold(p):
        q = p + pltpu.roll(p, 4, 0)
        q = q + pltpu.roll(q, 2, 0)
        out = q[:, 0:128]
        for j in range(1, 4):
            out = jnp.where(quarter == j, q[:, 128 * j : 128 * (j + 1)], out)
        return out

    def product(v8, matrix):
        wide = spread(v8)
        low = wide - wide.astype(jnp.bfloat16).astype(jnp.float32)
        stack = jnp.concatenate([wide, low], axis=0).astype(jnp.bfloat16)
        p = jnp.dot(stack, matrix, preferred_element_type=jnp.float32)
        return fold(p[0:8] + p[8:16])

    def rounded_product(v8, matrix):
        wide = spread(v8)
        stack = jnp.concatenate([wide, jnp.zeros_like(wide)], axis=0).astype(jnp.bfloat16)
        p = jnp.dot(stack, matrix, preferred_element_type=jnp.float32)
        return fold(p[0:8])

    def contribution(level):
        return rounded_product(solved[level], block[level])

    def combine(level):
        def half(step, carry):
            rows = pl.ds(pl.multiple_of(step * 256, 256), 256)
            both = jnp.dot(coupler[level, rows], inverse[level], preferred_element_type=jnp.float32)
            relay[level, rows] = both.astype(jnp.bfloat16)
            if level < levels - 1:
                onward = jnp.dot(relay[level, rows], block[level], preferred_element_type=jnp.float32)
                direct[level, rows] = onward.astype(jnp.bfloat16)
            return carry

        lax.fori_loop(0, 2, half, 0)

    strides, known = [], min(4, outer // 2)
    while known < outer // 2:
        strides.append(min(known, outer // 2 - known))
        known += strides[-1]

    def greet(step):
        for offset in sorted({strides[step], outer - strides[step]}):
            pl.semaphore_signal(meet.at[step], inc=1, device_id=z_peer(offset), device_id_type=MESH)

    def met(step):
        pl.semaphore_wait(meet.at[step], len({strides[step], outer - strides[step]}))

    pl.semaphore_wait(barrier, len(near) + INNER - 1 + 1)
    if strides:
        greet(0)

    def code_copy(offset):
        return pltpu.make_async_remote_copy(
            src_ref=code, dst_ref=codes.at[offset], send_sem=code_send, recv_sem=code_recv,
            device_id=y_peer(offset), device_id_type=MESH,
        )

    def x_copy(level):
        return pltpu.make_async_remote_copy(
            src_ref=solved.at[level], dst_ref=before.at[level], send_sem=x_send.at[level], recv_sem=x_recv.at[level],
            device_id={"grp": grp + 1}, device_id_type=MESH,
        )

    def y_copy(level, offset):
        return pltpu.make_async_remote_copy(
            src_ref=sent.at[level], dst_ref=yland.at[level, offset], send_sem=y_send.at[level],
            recv_sem=y_recv.at[level], device_id=y_peer(offset), device_id_type=MESH,
        )

    def z_copy(level, offset):
        return pltpu.make_async_remote_copy(
            src_ref=part.at[level, offset], dst_ref=zland.at[level, offset], send_sem=z_send.at[level],
            recv_sem=z_recv.at[level], device_id=z_peer(offset), device_id_type=MESH,
        )

    def bulk_wait(ref, sem):
        pltpu.make_async_copy(ref, ref, sem).wait()

    z_order, y_order = far_first(outer), far_first(INNER)

    def scatter(level):
        for offset in y_order:
            y_copy(level, offset).start()

    def total_of(terms):
        while len(terms) > 1:
            terms = [terms[i] + terms[i + 1] for i in range(0, len(terms) - 1, 2)] + terms[len(terms) & ~1 :]
        return terms[0]

    loads[0].wait()
    matrices[0]["D"].wait()
    for copy in loads[5:]:
        copy.start()
    solved[0] = product(rhs[0], inverse[0])

    @pl.when(grp == 0)
    def _():
        x_copy(0).start()

    matrices[0]["E"].wait()
    early[0] = contribution(0)
    loads[1].wait()
    both = route[0, 0] + 256 * route[0, 1]
    code[...] = jnp.full((1, 128), both, jnp.int32)
    codes[0] = code[...]

    @pl.when(grp == 0)
    def _():
        sent[0] = early[0].astype(jnp.bfloat16)
        scatter(0)

    if len(strides) > 1:
        met(0)
        for step in range(1, len(strides)):
            greet(step)
            if step < len(strides) - 1:
                met(step)
    for offset in y_order:
        code_copy(offset).start()
    matrices[0]["C"].wait()

    @pl.when(grp > 0)
    def _():
        combine(0)

    for level in range(levels):
        last = level == levels - 1
        if level > 0:
            bulk_wait(zland.at[level - 1, pl.ds(1, outer - 1)], z_recv.at[level - 1])
            incoming = total_of(
                [part[level - 1, 0].astype(jnp.float32)]
                + [zland[level - 1, offset].astype(jnp.float32) for offset in range(1, outer)]
            )
            solved[level] = product(rhs[level] - incoming, inverse[level])

            @pl.when(grp == 0)
            def _():
                x_copy(level).start()
                if not last:
                    sent[level] = contribution(level).astype(jnp.bfloat16)
                    scatter(level)

            if not last:
                @pl.when(grp > 0)
                def _():
                    early[level] = contribution(level)

        def absorb():
            solved[level] = solved[level] - product(before[level], relay[level])

        def pass_on():
            sent[level] = (early[level] - product(before[level], direct[level])).astype(jnp.bfloat16)
            scatter(level)

        @pl.when((grp > 0) & (grp < groups - 1))
        def _():
            bulk_wait(before.at[level], x_recv.at[level])
            absorb()
            x_copy(level).start()
            if not last:
                pass_on()

        @pl.when(grp == groups - 1)
        def _():
            bulk_wait(before.at[level], x_recv.at[level])
            if not last:
                pass_on()
            absorb()

        if last:
            break
        if level == 0:
            bulk_wait(codes.at[pl.ds(1, INNER - 1)], code_recv)
        bulk_wait(yland.at[level, pl.ds(1, INNER - 1)], y_recv.at[level])

        arrived = [sent[level].astype(jnp.float32)]
        arrived += [yland[level, offset].astype(jnp.float32) for offset in range(1, INNER)]
        marks = [jnp.broadcast_to(codes[offset], (8, 128)) for offset in range(INNER)]
        marks = [(mark // 256 if level else mark % 256) for mark in marks]

        def gathered(target):
            return total_of([jnp.where(mark == target, value, 0.0) for mark, value in zip(marks, arrived)])

        for offset in z_order + [0]:
            target = ((zpos + offset) % outer) * INNER + spot
            total = gathered(target)
            if level > 0:
                total = total + held[offset]
            part[level, offset] = total.astype(jnp.bfloat16)
            if level == 0 and strides and offset == z_order[0]:
                met(len(strides) - 1)
            if offset:
                z_copy(level, offset).start()
        if level == 0:
            for offset in range(outer):
                held[offset] = gathered(((zpos + offset) % outer) * INNER + spot + rowblocks)
            for copy in loads[5:]:
                copy.wait()

            @pl.when(grp > 0)
            def _():
                for later in range(1, levels):
                    combine(later)

    out_ref[...] = solved[...]

    bulk_wait(codes.at[pl.ds(1, INNER - 1)], code_send)
    for level in range(levels - 1):
        bulk_wait(yland.at[level, pl.ds(1, INNER - 1)], y_send.at[level])
        bulk_wait(zland.at[level, pl.ds(1, outer - 1)], z_send.at[level])

    @pl.when(grp < groups - 1)
    def _():
        for level in range(levels):
            bulk_wait(solved.at[level], x_send.at[level])


def shards(rhs, diag_inverse, coupling, off_block, off_route):
    groups = lax.axis_size("grp")
    outer = lax.axis_size("rows") // INNER
    levels, size = rhs.shape[0], rhs.shape[-1]
    assert levels == 3 and rhs.shape[-2:] == (2, 512)
    rows8 = rhs[:, 0, 0].reshape(levels, 2, 4, 128).transpose(0, 2, 1, 3).reshape(levels, 8, 128)
    hbm = pl.BlockSpec(memory_space=pl.ANY)
    dma = pltpu.SemaphoreType.DMA
    out = pl.pallas_call(
        functools.partial(kernel, outer, groups),
        out_shape=pltpu.VMEM((levels, 8, 128), jnp.float32),
        in_specs=[hbm] * 5,
        out_specs=pl.BlockSpec(memory_space=pltpu.VMEM),
        scratch_shapes=[
            pltpu.VMEM((levels, 8, 128), jnp.float32),
            pltpu.VMEM((levels, size, size), jnp.bfloat16),
            pltpu.VMEM((levels, size, size), jnp.bfloat16),
            pltpu.VMEM((levels - 1, size, size), jnp.bfloat16),
            pltpu.SMEM((1, levels - 1), jnp.int32),
            pltpu.VMEM((1, 128), jnp.int32),
            pltpu.VMEM((INNER, 1, 128), jnp.int32),
            pltpu.VMEM((levels, 8, 128), jnp.float32),
            pltpu.VMEM((levels, 8, 128), jnp.float32),
            pltpu.VMEM((levels - 1, 8, 128), jnp.bfloat16),
            pltpu.VMEM((levels - 1, 8, 128), jnp.float32),
            pltpu.VMEM((levels, size, size), jnp.bfloat16),
            pltpu.VMEM((levels - 1, size, size), jnp.bfloat16),
            pltpu.VMEM((levels - 1, INNER, 8, 128), jnp.bfloat16),
            pltpu.VMEM((outer, 8, 128), jnp.float32),
            pltpu.VMEM((levels - 1, outer, 8, 128), jnp.bfloat16),
            pltpu.VMEM((levels - 1, outer, 8, 128), jnp.bfloat16),
            dma((2 + 3 * levels - 1,)),
            pltpu.SemaphoreType.REGULAR((max(1, outer.bit_length() - 2),)),
            dma, dma,
            dma((levels,)), dma((levels,)),
            dma((levels - 1,)), dma((levels - 1,)),
            dma((levels - 1,)), dma((levels - 1,)),
        ],
        compiler_params=pltpu.CompilerParams(collective_id=0, has_side_effects=True),
    )(rows8, diag_inverse[:, 0, 0], coupling[:, 0, 0], off_block[:, 0, 0], off_route[:, 0].T)
    out = out.reshape(levels, 4, 2, 128).transpose(0, 2, 1, 3).reshape(levels, 2, size)
    return out[:, None, None]


def solution(mesh):
    return jax.shard_map(
        shards,
        mesh=mesh,
        in_specs=(
            P(None, "rows", "grp", None, None),
            P(None, "rows", "grp", None, None),
            P(None, "rows", "grp", None, None),
            P(None, "rows", "grp", None, None),
            P(None, "rows", "grp"),
        ),
        out_specs=P(None, "rows", "grp", None, None),
        check_vma=False,
    )
```

```python
import functools

import jax
import jax.numpy as jnp
from jax import lax
from jax.experimental import pallas as pl
from jax.experimental.pallas import tpu as pltpu
from jax.sharding import PartitionSpec as P

INNER = 8
MESH = pl.DeviceIdType.MESH


def far_first(count):
    return sorted(range(1, count), key=lambda offset: -min(offset, count - offset))


def kernel(
    outer, groups, rhs_hbm, inverse_hbm, coupler_hbm, block_hbm, route_hbm, out_ref,
    rhs, inverse, coupler, block, route, code, codes, solved, before, sent, early, relay, direct, yland, held, part, zland,
    in_sem, meet, code_send, code_recv, x_send, x_recv, y_send, y_recv, z_send, z_recv,
):
    levels = rhs.shape[0]
    rowblocks = outer * INNER
    row = lax.axis_index("rows")
    grp = lax.axis_index("grp")
    zpos = row // INNER
    spot = row % INNER

    def z_peer(offset):
        return {"rows": ((zpos + offset) % outer) * INNER + spot}

    def y_peer(offset):
        return {"rows": zpos * INNER + (spot + offset) % INNER}

    barrier = pltpu.get_barrier_semaphore()
    near = sorted({offset % outer for offset in (4, -4, 3, -3, 2, -2, 1, -1)} - {0}, key=lambda offset: -min(offset, outer - offset))
    for offset in near:
        pl.semaphore_signal(barrier, inc=1, device_id=z_peer(offset), device_id_type=MESH)
    for offset in far_first(INNER):
        pl.semaphore_signal(barrier, inc=1, device_id=y_peer(offset), device_id_type=MESH)
    left = {"grp": (grp + groups - 1) % groups}
    pl.semaphore_signal(barrier, inc=1, device_id=left, device_id_type=MESH)

    loads = [pltpu.make_async_copy(rhs_hbm, rhs, in_sem.at[0]), pltpu.make_async_copy(route_hbm, route, in_sem.at[1])]
    index = 2
    matrices = []
    for level in range(levels):
        entry = {}
        for name, source, target in (("D", inverse_hbm, inverse), ("E", block_hbm, block), ("C", coupler_hbm, coupler)):
            if name == "E" and level == levels - 1:
                continue
            copy = pltpu.make_async_copy(source.at[level], target.at[level], in_sem.at[index])
            index += 1
            loads.append(copy)
            entry[name] = copy
        matrices.append(entry)
    first = loads[:5]
    for copy in first:
        copy.start()

    quarter = lax.broadcasted_iota(jnp.int32, (8, 128), 0) // 2

    def spread(v8):
        return jnp.concatenate([jnp.where(quarter == j, v8, 0.0) for j in range(4)], axis=1)

    def fold(p):
        q = p + pltpu.roll(p, 4, 0)
        q = q + pltpu.roll(q, 2, 0)
        out = q[:, 0:128]
        for j in range(1, 4):
            out = jnp.where(quarter == j, q[:, 128 * j : 128 * (j + 1)], out)
        return out

    def product(v8, matrix):
        wide = spread(v8)
        low = wide - wide.astype(jnp.bfloat16).astype(jnp.float32)
        stack = jnp.concatenate([wide, low], axis=0).astype(jnp.bfloat16)
        p = jnp.dot(stack, matrix, preferred_element_type=jnp.float32)
        return fold(p[0:8] + p[8:16])

    def rounded_product(v8, matrix):
        wide = spread(v8)
        stack = jnp.concatenate([wide, jnp.zeros_like(wide)], axis=0).astype(jnp.bfloat16)
        p = jnp.dot(stack, matrix, preferred_element_type=jnp.float32)
        return fold(p[0:8])

    def contribution(level):
        return rounded_product(solved[level], block[level])

    def combine(level):
        def half(step, carry):
            rows = pl.ds(pl.multiple_of(step * 256, 256), 256)
            both = jnp.dot(coupler[level, rows], inverse[level], preferred_element_type=jnp.float32)
            relay[level, rows] = both.astype(jnp.bfloat16)
            if level < levels - 1:
                onward = jnp.dot(relay[level, rows], block[level], preferred_element_type=jnp.float32)
                direct[level, rows] = onward.astype(jnp.bfloat16)
            return carry

        lax.fori_loop(0, 2, half, 0)

    strides, known = [], min(4, outer // 2)
    while known < outer // 2:
        strides.append(min(known, outer // 2 - known))
        known += strides[-1]

    def greet(step):
        for offset in sorted({strides[step], outer - strides[step]}):
            pl.semaphore_signal(meet.at[step], inc=1, device_id=z_peer(offset), device_id_type=MESH)

    def met(step):
        pl.semaphore_wait(meet.at[step], len({strides[step], outer - strides[step]}))

    def code_copy(offset):
        return pltpu.make_async_remote_copy(
            src_ref=code, dst_ref=codes.at[offset], send_sem=code_send, recv_sem=code_recv,
            device_id=y_peer(offset), device_id_type=MESH,
        )

    def x_copy(level):
        return pltpu.make_async_remote_copy(
            src_ref=solved.at[level], dst_ref=before.at[level], send_sem=x_send.at[level], recv_sem=x_recv.at[level],
            device_id={"grp": grp + 1}, device_id_type=MESH,
        )

    def y_copy(level, offset):
        return pltpu.make_async_remote_copy(
            src_ref=sent.at[level], dst_ref=yland.at[level, offset], send_sem=y_send.at[level],
            recv_sem=y_recv.at[level], device_id=y_peer(offset), device_id_type=MESH,
        )

    def z_copy(level, offset):
        return pltpu.make_async_remote_copy(
            src_ref=part.at[level, offset], dst_ref=zland.at[level, offset], send_sem=z_send.at[level],
            recv_sem=z_recv.at[level], device_id=z_peer(offset), device_id_type=MESH,
        )

    def bulk_wait(ref, sem):
        pltpu.make_async_copy(ref, ref, sem).wait()

    z_order, y_order = far_first(outer), far_first(INNER)

    def scatter(level):
        for offset in y_order:
            y_copy(level, offset).start()

    def total_of(terms):
        while len(terms) > 1:
            terms = [terms[i] + terms[i + 1] for i in range(0, len(terms) - 1, 2)] + terms[len(terms) & ~1 :]
        return terms[0]

    loads[0].wait()
    matrices[0]["D"].wait()
    for copy in loads[5:]:
        copy.start()
    solved[0] = product(rhs[0], inverse[0])
    loads[1].wait()
    both = route[0, 0] + 256 * route[0, 1]
    code[...] = jnp.full((1, 128), both, jnp.int32)
    codes[0] = code[...]
    matrices[0]["E"].wait()
    early[0] = contribution(0)
    sent[0] = early[0].astype(jnp.bfloat16)

    pl.semaphore_wait(barrier, len(near) + INNER - 1 + 1)
    if strides:
        greet(0)

    @pl.when(grp == 0)
    def _():
        x_copy(0).start()

    for offset in y_order:
        code_copy(offset).start()

    @pl.when(grp == 0)
    def _():
        scatter(0)

    if len(strides) > 1:
        met(0)
        for step in range(1, len(strides)):
            greet(step)
            if step < len(strides) - 1:
                met(step)
    matrices[0]["C"].wait()

    @pl.when(grp > 0)
    def _():
        combine(0)

    for level in range(levels):
        last = level == levels - 1
        if level > 0:
            bulk_wait(zland.at[level - 1, pl.ds(1, outer - 1)], z_recv.at[level - 1])
            incoming = total_of(
                [part[level - 1, 0].astype(jnp.float32)]
                + [zland[level - 1, offset].astype(jnp.float32) for offset in range(1, outer)]
            )
            solved[level] = product(rhs[level] - incoming, inverse[level])

            @pl.when(grp == 0)
            def _():
                x_copy(level).start()
                if not last:
                    sent[level] = contribution(level).astype(jnp.bfloat16)
                    scatter(level)

            if not last:
                @pl.when(grp > 0)
                def _():
                    early[level] = contribution(level)

        def absorb():
            solved[level] = solved[level] - product(before[level], relay[level])

        def pass_on():
            sent[level] = (early[level] - product(before[level], direct[level])).astype(jnp.bfloat16)
            scatter(level)

        @pl.when((grp > 0) & (grp < groups - 1))
        def _():
            bulk_wait(before.at[level], x_recv.at[level])
            absorb()
            x_copy(level).start()
            if not last:
                pass_on()

        @pl.when(grp == groups - 1)
        def _():
            bulk_wait(before.at[level], x_recv.at[level])
            if not last:
                pass_on()
            absorb()

        if last:
            break
        if level == 0:
            bulk_wait(codes.at[pl.ds(1, INNER - 1)], code_recv)
        bulk_wait(yland.at[level, pl.ds(1, INNER - 1)], y_recv.at[level])

        arrived = [sent[level].astype(jnp.float32)]
        arrived += [yland[level, offset].astype(jnp.float32) for offset in range(1, INNER)]
        marks = [jnp.broadcast_to(codes[offset], (8, 128)) for offset in range(INNER)]
        marks = [(mark // 256 if level else mark % 256) for mark in marks]

        def gathered(target):
            return total_of([jnp.where(mark == target, value, 0.0) for mark, value in zip(marks, arrived)])

        for offset in z_order + [0]:
            target = ((zpos + offset) % outer) * INNER + spot
            total = gathered(target)
            if level > 0:
                total = total + held[offset]
            part[level, offset] = total.astype(jnp.bfloat16)
            if level == 0 and strides and offset == z_order[0]:
                met(len(strides) - 1)
            if offset:
                z_copy(level, offset).start()
        if level == 0:
            for offset in range(outer):
                held[offset] = gathered(((zpos + offset) % outer) * INNER + spot + rowblocks)
            for copy in loads[5:]:
                copy.wait()

            @pl.when(grp > 0)
            def _():
                for later in range(1, levels):
                    combine(later)

    out_ref[...] = solved[...]

    bulk_wait(codes.at[pl.ds(1, INNER - 1)], code_send)
    for level in range(levels - 1):
        bulk_wait(yland.at[level, pl.ds(1, INNER - 1)], y_send.at[level])
        bulk_wait(zland.at[level, pl.ds(1, outer - 1)], z_send.at[level])

    @pl.when(grp < groups - 1)
    def _():
        for level in range(levels):
            bulk_wait(solved.at[level], x_send.at[level])


def shards(rhs, diag_inverse, coupling, off_block, off_route):
    groups = lax.axis_size("grp")
    outer = lax.axis_size("rows") // INNER
    levels, size = rhs.shape[0], rhs.shape[-1]
    assert levels == 3 and rhs.shape[-2:] == (2, 512)
    rows8 = rhs[:, 0, 0].reshape(levels, 2, 4, 128).transpose(0, 2, 1, 3).reshape(levels, 8, 128)
    hbm = pl.BlockSpec(memory_space=pl.ANY)
    dma = pltpu.SemaphoreType.DMA
    out = pl.pallas_call(
        functools.partial(kernel, outer, groups),
        out_shape=pltpu.VMEM((levels, 8, 128), jnp.float32),
        in_specs=[hbm] * 5,
        out_specs=pl.BlockSpec(memory_space=pltpu.VMEM),
        scratch_shapes=[
            pltpu.VMEM((levels, 8, 128), jnp.float32),
            pltpu.VMEM((levels, size, size), jnp.bfloat16),
            pltpu.VMEM((levels, size, size), jnp.bfloat16),
            pltpu.VMEM((levels - 1, size, size), jnp.bfloat16),
            pltpu.SMEM((1, levels - 1), jnp.int32),
            pltpu.VMEM((1, 128), jnp.int32),
            pltpu.VMEM((INNER, 1, 128), jnp.int32),
            pltpu.VMEM((levels, 8, 128), jnp.float32),
            pltpu.VMEM((levels, 8, 128), jnp.float32),
            pltpu.VMEM((levels - 1, 8, 128), jnp.bfloat16),
            pltpu.VMEM((levels - 1, 8, 128), jnp.float32),
            pltpu.VMEM((levels, size, size), jnp.bfloat16),
            pltpu.VMEM((levels - 1, size, size), jnp.bfloat16),
            pltpu.VMEM((levels - 1, INNER, 8, 128), jnp.bfloat16),
            pltpu.VMEM((outer, 8, 128), jnp.float32),
            pltpu.VMEM((levels - 1, outer, 8, 128), jnp.bfloat16),
            pltpu.VMEM((levels - 1, outer, 8, 128), jnp.bfloat16),
            dma((2 + 3 * levels - 1,)),
            pltpu.SemaphoreType.REGULAR((max(1, outer.bit_length() - 2),)),
            dma, dma,
            dma((levels,)), dma((levels,)),
            dma((levels - 1,)), dma((levels - 1,)),
            dma((levels - 1,)), dma((levels - 1,)),
        ],
        compiler_params=pltpu.CompilerParams(collective_id=0, has_side_effects=True),
    )(rows8, diag_inverse[:, 0, 0], coupling[:, 0, 0], off_block[:, 0, 0], off_route[:, 0].T)
    out = out.reshape(levels, 4, 2, 128).transpose(0, 2, 1, 3).reshape(levels, 2, size)
    return out[:, None, None]


def solution(mesh):
    return jax.shard_map(
        shards,
        mesh=mesh,
        in_specs=(
            P(None, "rows", "grp", None, None),
            P(None, "rows", "grp", None, None),
            P(None, "rows", "grp", None, None),
            P(None, "rows", "grp", None, None),
            P(None, "rows", "grp"),
        ),
        out_specs=P(None, "rows", "grp", None, None),
        check_vma=False,
    )
```

```python
import functools

import jax
import jax.numpy as jnp
from jax import lax
from jax.experimental import pallas as pl
from jax.experimental.pallas import tpu as pltpu
from jax.sharding import PartitionSpec as P

INNER = 8
MESH = pl.DeviceIdType.MESH


def far_first(count):
    return sorted(range(1, count), key=lambda offset: -min(offset, count - offset))


def kernel(
    outer, groups, rhs_hbm, inverse_hbm, coupler_hbm, block_hbm, route_hbm, out_ref,
    rhs, inverse, coupler, block, route, code, codes, solved, before, sent, early, relay, direct, yland, held, part, zland,
    in_sem, meet, code_send, code_recv, x_send, x_recv, y_send, y_recv, z_send, z_recv,
):
    levels = rhs.shape[0]
    rowblocks = outer * INNER
    row = lax.axis_index("rows")
    grp = lax.axis_index("grp")
    zpos = row // INNER
    spot = row % INNER

    def z_peer(offset):
        return {"rows": ((zpos + offset) % outer) * INNER + spot}

    def y_peer(offset):
        return {"rows": zpos * INNER + (spot + offset) % INNER}

    barrier = pltpu.get_barrier_semaphore()
    near = sorted({offset % outer for offset in (4, -4, 3, -3, 2, -2, 1, -1)} - {0}, key=lambda offset: -min(offset, outer - offset))
    for offset in near:
        pl.semaphore_signal(barrier, inc=1, device_id=z_peer(offset), device_id_type=MESH)
    for offset in far_first(INNER):
        pl.semaphore_signal(barrier, inc=1, device_id=y_peer(offset), device_id_type=MESH)
    left = {"grp": (grp + groups - 1) % groups}
    pl.semaphore_signal(barrier, inc=1, device_id=left, device_id_type=MESH)

    loads = [pltpu.make_async_copy(rhs_hbm, rhs, in_sem.at[0]), pltpu.make_async_copy(route_hbm, route, in_sem.at[1])]
    index = 2
    matrices = []
    for level in range(levels):
        entry = {}
        for name, source, target in (("D", inverse_hbm, inverse), ("E", block_hbm, block), ("C", coupler_hbm, coupler)):
            if name == "E" and level == levels - 1:
                continue
            copy = pltpu.make_async_copy(source.at[level], target.at[level], in_sem.at[index])
            index += 1
            loads.append(copy)
            entry[name] = copy
        matrices.append(entry)
    first = loads[:5]
    for copy in first:
        copy.start()

    quarter = lax.broadcasted_iota(jnp.int32, (8, 128), 0) // 2

    def spread(v8):
        return jnp.concatenate([jnp.where(quarter == j, v8, 0.0) for j in range(4)], axis=1)

    def fold(p):
        q = p + pltpu.roll(p, 4, 0)
        q = q + pltpu.roll(q, 2, 0)
        out = q[:, 0:128]
        for j in range(1, 4):
            out = jnp.where(quarter == j, q[:, 128 * j : 128 * (j + 1)], out)
        return out

    def product(v8, matrix):
        wide = spread(v8)
        low = wide - wide.astype(jnp.bfloat16).astype(jnp.float32)
        stack = jnp.concatenate([wide, low], axis=0).astype(jnp.bfloat16)
        p = jnp.dot(stack, matrix, preferred_element_type=jnp.float32)
        return fold(p[0:8] + p[8:16])

    def rounded_product(v8, matrix):
        wide = spread(v8)
        stack = jnp.concatenate([wide, jnp.zeros_like(wide)], axis=0).astype(jnp.bfloat16)
        p = jnp.dot(stack, matrix, preferred_element_type=jnp.float32)
        return fold(p[0:8])

    def contribution(level):
        return rounded_product(solved[level], block[level])

    def combine(level):
        def half(step, carry):
            rows = pl.ds(pl.multiple_of(step * 256, 256), 256)
            both = jnp.dot(coupler[level, rows], inverse[level], preferred_element_type=jnp.float32)
            relay[level, rows] = both.astype(jnp.bfloat16)
            if level < levels - 1:
                onward = jnp.dot(relay[level, rows], block[level], preferred_element_type=jnp.float32)
                direct[level, rows] = onward.astype(jnp.bfloat16)
            return carry

        lax.fori_loop(0, 2, half, 0)

    strides, known = [], min(4, outer // 2)
    while known < outer // 2:
        strides.append(min(known, outer // 2 - known))
        known += strides[-1]

    def greet(step):
        for offset in sorted({strides[step], outer - strides[step]}):
            pl.semaphore_signal(meet.at[step], inc=1, device_id=z_peer(offset), device_id_type=MESH)

    def met(step):
        pl.semaphore_wait(meet.at[step], len({strides[step], outer - strides[step]}))

    def code_copy(offset):
        return pltpu.make_async_remote_copy(
            src_ref=code, dst_ref=codes.at[offset], send_sem=code_send, recv_sem=code_recv,
            device_id=y_peer(offset), device_id_type=MESH,
        )

    def x_copy(level):
        return pltpu.make_async_remote_copy(
            src_ref=solved.at[level], dst_ref=before.at[level], send_sem=x_send.at[level], recv_sem=x_recv.at[level],
            device_id={"grp": grp + 1}, device_id_type=MESH,
        )

    def y_copy(level, offset):
        return pltpu.make_async_remote_copy(
            src_ref=sent.at[level], dst_ref=yland.at[level, offset], send_sem=y_send.at[level],
            recv_sem=y_recv.at[level], device_id=y_peer(offset), device_id_type=MESH,
        )

    def z_copy(level, offset):
        return pltpu.make_async_remote_copy(
            src_ref=part.at[level, offset], dst_ref=zland.at[level, offset], send_sem=z_send.at[level],
            recv_sem=z_recv.at[level], device_id=z_peer(offset), device_id_type=MESH,
        )

    def bulk_wait(ref, sem):
        pltpu.make_async_copy(ref, ref, sem).wait()

    z_order, y_order = far_first(outer), far_first(INNER)

    def scatter(level):
        for offset in y_order:
            y_copy(level, offset).start()

    def total_of(terms):
        while len(terms) > 1:
            terms = [terms[i] + terms[i + 1] for i in range(0, len(terms) - 1, 2)] + terms[len(terms) & ~1 :]
        return terms[0]

    loads[0].wait()
    matrices[0]["D"].wait()
    for copy in loads[5:]:
        copy.start()
    solved[0] = product(rhs[0], inverse[0])
    loads[1].wait()
    both = route[0, 0] + 256 * route[0, 1]
    code[...] = jnp.full((1, 128), both, jnp.int32)
    codes[0] = code[...]
    matrices[0]["E"].wait()
    early[0] = contribution(0)
    sent[0] = early[0].astype(jnp.bfloat16)

    pl.semaphore_wait(barrier, len(near) + INNER - 1 + 1)
    if strides:
        greet(0)

    @pl.when(grp == 0)
    def _():
        scatter(0)

    for offset in y_order:
        code_copy(offset).start()

    @pl.when(grp == 0)
    def _():
        x_copy(0).start()

    if len(strides) > 1:
        met(0)
        for step in range(1, len(strides)):
            greet(step)
            if step < len(strides) - 1:
                met(step)
    matrices[0]["C"].wait()

    @pl.when(grp > 0)
    def _():
        combine(0)

    for level in range(levels):
        last = level == levels - 1
        if level > 0:
            bulk_wait(zland.at[level - 1, pl.ds(1, outer - 1)], z_recv.at[level - 1])
            incoming = total_of(
                [part[level - 1, 0].astype(jnp.float32)]
                + [zland[level - 1, offset].astype(jnp.float32) for offset in range(1, outer)]
            )
            solved[level] = product(rhs[level] - incoming, inverse[level])

            @pl.when(grp == 0)
            def _():
                x_copy(level).start()
                if not last:
                    sent[level] = contribution(level).astype(jnp.bfloat16)
                    scatter(level)

            if not last:
                @pl.when(grp > 0)
                def _():
                    early[level] = contribution(level)

        def absorb():
            solved[level] = solved[level] - product(before[level], relay[level])

        def pass_on():
            sent[level] = (early[level] - product(before[level], direct[level])).astype(jnp.bfloat16)
            scatter(level)

        @pl.when((grp > 0) & (grp < groups - 1))
        def _():
            bulk_wait(before.at[level], x_recv.at[level])
            absorb()
            x_copy(level).start()
            if not last:
                pass_on()

        @pl.when(grp == groups - 1)
        def _():
            bulk_wait(before.at[level], x_recv.at[level])
            if not last:
                pass_on()
            absorb()

        if last:
            break
        if level == 0:
            bulk_wait(codes.at[pl.ds(1, INNER - 1)], code_recv)
        bulk_wait(yland.at[level, pl.ds(1, INNER - 1)], y_recv.at[level])

        arrived = [sent[level].astype(jnp.float32)]
        arrived += [yland[level, offset].astype(jnp.float32) for offset in range(1, INNER)]
        marks = [jnp.broadcast_to(codes[offset], (8, 128)) for offset in range(INNER)]
        marks = [(mark // 256 if level else mark % 256) for mark in marks]

        def gathered(target):
            return total_of([jnp.where(mark == target, value, 0.0) for mark, value in zip(marks, arrived)])

        for offset in z_order + [0]:
            target = ((zpos + offset) % outer) * INNER + spot
            total = gathered(target)
            if level > 0:
                total = total + held[offset]
            part[level, offset] = total.astype(jnp.bfloat16)
            if level == 0 and strides and offset == z_order[0]:
                met(len(strides) - 1)
            if offset:
                z_copy(level, offset).start()
        if level == 0:
            for offset in range(outer):
                held[offset] = gathered(((zpos + offset) % outer) * INNER + spot + rowblocks)
            for copy in loads[5:]:
                copy.wait()

            @pl.when(grp > 0)
            def _():
                for later in range(1, levels):
                    combine(later)

    out_ref[...] = solved[...]

    bulk_wait(codes.at[pl.ds(1, INNER - 1)], code_send)
    for level in range(levels - 1):
        bulk_wait(yland.at[level, pl.ds(1, INNER - 1)], y_send.at[level])
        bulk_wait(zland.at[level, pl.ds(1, outer - 1)], z_send.at[level])

    @pl.when(grp < groups - 1)
    def _():
        for level in range(levels):
            bulk_wait(solved.at[level], x_send.at[level])


def shards(rhs, diag_inverse, coupling, off_block, off_route):
    groups = lax.axis_size("grp")
    outer = lax.axis_size("rows") // INNER
    levels, size = rhs.shape[0], rhs.shape[-1]
    assert levels == 3 and rhs.shape[-2:] == (2, 512)
    rows8 = rhs[:, 0, 0].reshape(levels, 2, 4, 128).transpose(0, 2, 1, 3).reshape(levels, 8, 128)
    hbm = pl.BlockSpec(memory_space=pl.ANY)
    dma = pltpu.SemaphoreType.DMA
    out = pl.pallas_call(
        functools.partial(kernel, outer, groups),
        out_shape=pltpu.VMEM((levels, 8, 128), jnp.float32),
        in_specs=[hbm] * 5,
        out_specs=pl.BlockSpec(memory_space=pltpu.VMEM),
        scratch_shapes=[
            pltpu.VMEM((levels, 8, 128), jnp.float32),
            pltpu.VMEM((levels, size, size), jnp.bfloat16),
            pltpu.VMEM((levels, size, size), jnp.bfloat16),
            pltpu.VMEM((levels - 1, size, size), jnp.bfloat16),
            pltpu.SMEM((1, levels - 1), jnp.int32),
            pltpu.VMEM((1, 128), jnp.int32),
            pltpu.VMEM((INNER, 1, 128), jnp.int32),
            pltpu.VMEM((levels, 8, 128), jnp.float32),
            pltpu.VMEM((levels, 8, 128), jnp.float32),
            pltpu.VMEM((levels - 1, 8, 128), jnp.bfloat16),
            pltpu.VMEM((levels - 1, 8, 128), jnp.float32),
            pltpu.VMEM((levels, size, size), jnp.bfloat16),
            pltpu.VMEM((levels - 1, size, size), jnp.bfloat16),
            pltpu.VMEM((levels - 1, INNER, 8, 128), jnp.bfloat16),
            pltpu.VMEM((outer, 8, 128), jnp.float32),
            pltpu.VMEM((levels - 1, outer, 8, 128), jnp.bfloat16),
            pltpu.VMEM((levels - 1, outer, 8, 128), jnp.bfloat16),
            dma((2 + 3 * levels - 1,)),
            pltpu.SemaphoreType.REGULAR((max(1, outer.bit_length() - 2),)),
            dma, dma,
            dma((levels,)), dma((levels,)),
            dma((levels - 1,)), dma((levels - 1,)),
            dma((levels - 1,)), dma((levels - 1,)),
        ],
        compiler_params=pltpu.CompilerParams(collective_id=0, has_side_effects=True),
    )(rows8, diag_inverse[:, 0, 0], coupling[:, 0, 0], off_block[:, 0, 0], off_route[:, 0].T)
    out = out.reshape(levels, 4, 2, 128).transpose(0, 2, 1, 3).reshape(levels, 2, size)
    return out[:, None, None]


def solution(mesh):
    return jax.shard_map(
        shards,
        mesh=mesh,
        in_specs=(
            P(None, "rows", "grp", None, None),
            P(None, "rows", "grp", None, None),
            P(None, "rows", "grp", None, None),
            P(None, "rows", "grp", None, None),
            P(None, "rows", "grp"),
        ),
        out_specs=P(None, "rows", "grp", None, None),
        check_vma=False,
    )
```
